32 devices in a mesh: var: 16 (over z, y, core), samp: 2 (over x).
Axes of the slice: x: 2, y: 2, z: 4, core: 2. Of those that a mesh axis runs over, the one named last changes fastest.
Arguments:
- genotypes: bfloat16 [4096, 12288], P('samp', 'var'), may hold values from -6 to 6
- marginal: float32 [12288, 1024], P('var', 'samp'), may hold values from -6 to 6
- start_effects: float32 [12288, 1024], P('var', 'samp'), may hold values from -5 to 5
- thresholds: float32 [1024], P('samp'), may hold values from 0.02 to 0.5
Outputs:
- shrunk_effects: float32 [12288, 1024], P('var', 'samp')
The draws below stay inside these ranges and needn't reach their ends.
All inputs are finite; a program needn't handle non-finite values.
Results may differ from the reference program's by a relative error of at most 0.0003.
Values may be sent and summed in bfloat16 or wider, within the bound.
A program may use at most 64 MiB of HBM per device.

```python
import math
import jax
import jax.numpy as jnp
from jax import lax

TILE = 256
TRAITS = 1024
SWEEPS = 2
VARIANTS = 12288
NSAMP = 4096


def level_of(stream_key, extent, shards, least, top_value):
    def one(position, parts):
        heights = jax.random.uniform(jax.random.fold_in(jax.random.fold_in(stream_key, 6), position), (parts,), jnp.float32, least / len(shards), top_value / len(shards))
        return jnp.repeat(jnp.exp(heights), extent[position] // parts).reshape((-1,) + (1,) * (len(extent) - position - 1))

    factor_of = one(*shards[0])
    for cut in shards[1:]:
        factor_of = factor_of * one(*cut)
    return factor_of


def bell_draw(key, extent, width, most, pieces=(), held_as=jnp.bfloat16):
    loudness = level_of(key, extent, pieces, -0.22, 0.18) if pieces else 1.0
    entries = jax.random.normal(key, extent, jnp.float32) * width * loudness
    return jnp.minimum(jnp.maximum(entries, -most), most).astype(held_as)


def setup_inputs(seed: int = 0) -> dict:
    keys = jax.random.split(jax.random.key(seed), 5)
    return {
        "genotypes": bell_draw(keys[0], (NSAMP, VARIANTS), 1.0, 6.0, ((0, 2), (1, 16))),
        "marginal": bell_draw(keys[1], (VARIANTS, TRAITS), 1.0, 6.0, ((0, 16), (1, 2)), jnp.float32),
        "start_effects": bell_draw(keys[2], (VARIANTS, TRAITS), 0.7, 5.0, ((0, 16), (1, 2)), jnp.float32),
        "thresholds": jnp.clip(jnp.exp(math.log(0.5) - 3.218876 * jax.random.uniform(keys[3], (TRAITS,), jnp.float32) ** level_of(keys[3], (TRAITS,), ((0, 2),), -0.2, 0.2)), 0.02, 0.5),
    }


shrinkage = 0.2


def reference(genotypes, marginal, start_effects, thresholds):
    tile_count = VARIANTS // TILE

    def gram_tile(index):
        left_tile = lax.dynamic_slice_in_dim(genotypes, index * TILE, TILE, 1).astype(jnp.float32)
        right_start = jnp.minimum(index + 1, tile_count - 1).astype(jnp.int32) * TILE
        right_tile = lax.dynamic_slice_in_dim(genotypes, right_start, TILE, 1).astype(jnp.float32)
        paired = jnp.concatenate([left_tile, right_tile], axis=1)
        return lax.dot_general(left_tile, paired, (((0,), (0,)), ((), ())), preferred_element_type=jnp.float32)

    products = lax.map(gram_tile, jnp.arange(tile_count, dtype=jnp.int32)) / NSAMP
    diag_tiles = products[:, :, :TILE]
    keep_upper = (jnp.arange(tile_count) < tile_count - 1).astype(jnp.float32)
    upper_tiles = products[:, :, TILE:] * keep_upper[:, None, None]
    lower_tiles = jnp.concatenate([jnp.zeros((1, TILE, TILE), jnp.float32), jnp.transpose(upper_tiles[:-1], (0, 2, 1))], axis=0)
    ld_diagonal = jnp.diagonal(diag_tiles, axis1=1, axis2=2).reshape(VARIANTS)
    divisor = (1.0 - shrinkage) * ld_diagonal + shrinkage
    limit_rows = thresholds[None, :]
    effects = start_effects
    empty = jnp.zeros((1, TILE, TRAITS), jnp.float32)
    high = lax.Precision.HIGHEST
    for sweep_index in range(SWEEPS):
        blocks = effects.reshape(tile_count, TILE, TRAITS)
        earlier = jnp.concatenate([empty, blocks[:-1]], axis=0)
        following = jnp.concatenate([blocks[1:], empty], axis=0)
        combined = jnp.einsum("tij,tjk->tik", diag_tiles, blocks, precision=high)
        combined = combined + jnp.einsum("tij,tjk->tik", lower_tiles, earlier, precision=high)
        combined = combined + jnp.einsum("tij,tjk->tik", upper_tiles, following, precision=high)
        combined = combined.reshape(VARIANTS, TRAITS)
        cross_term = (1.0 - shrinkage) * (combined - ld_diagonal[:, None] * effects)
        adjusted = marginal - cross_term
        effects = (adjusted - jnp.clip(adjusted, -limit_rows, limit_rows)) / divisor[:, None]
    return effects
```

```python
import functools

import jax
import jax.numpy as jnp
from jax import lax
from jax.experimental import pallas as pl
from jax.experimental.pallas import tpu as pltpu
from jax.sharding import PartitionSpec as P

TILE = 256
HALF = TILE // 2
SWEEPS = 2
LD_SCALE = 1024.0

shrinkage = 0.2
MESH = pl.DeviceIdType.MESH
F32 = jnp.float32
BF16 = jnp.bfloat16


def encode(value):
    square = value * value
    fourth = square * square
    eighth = fourth * fourth
    return jnp.where(value < 0, -eighth, eighth).astype(BF16)


def decode(code):
    code = code.astype(F32)
    root = jnp.sqrt(jnp.sqrt(jnp.sqrt(jnp.abs(code))))
    return jnp.where(code < 0, -root, root)


def split(value):
    high = value.astype(BF16)
    return high, (value - high.astype(F32)).astype(BF16)


def iota_pair(size):
    row = lax.broadcasted_iota(jnp.int32, (size, size), 0)
    col = lax.broadcasted_iota(jnp.int32, (size, size), 1)
    return row, col


def pack_symmetric(tile):
    row, col = iota_pair(HALF)
    mixed = jnp.where(row < col, tile[:HALF, :HALF], tile[HALF:, HALF:])
    return jnp.concatenate([mixed, tile[:HALF, HALF:]], axis=1)


def unpack_symmetric(packed):
    row, col = iota_pair(HALF)
    mixed, corner = packed[:, :HALF], packed[:, HALF:]
    upper = jnp.where(row < col, mixed, 0.0)
    lower = jnp.where(row > col, mixed, 0.0)
    first = jnp.concatenate([upper + upper.T, corner], axis=1)
    second = jnp.concatenate([corner.T, lower + lower.T], axis=1)
    return jnp.concatenate([first, second], axis=0)


def gram(left, right):
    return lax.dot_general(left, right, (((0,), (0,)), ((), ())), preferred_element_type=F32)


def kernel(
    tiles, var_size, samp_size, inv_total,
    geno_hbm, marg_hbm, start_hbm, limit_ref, out_hbm,
    geno, halo, marg, start, own, code, got, diag, diag_got,
    band_hi, band_lo, eff_hi, eff_lo, edge_code, edge_got, cross_code, cross_got, result,
    load_sem, store_sem, geno_sem, part_send, part_recv, cross_sem, edge_send, edge_recv,
):
    var = lax.axis_index("var")
    samp = lax.axis_index("samp")
    has_prev = var > 0
    has_next = var < var_size - 1
    prev, following = var - 1, var + 1
    peers = [lax.rem(samp + k, samp_size) for k in range(1, samp_size)]
    last = tiles - 1
    columns = geno.shape[1]

    step = HALF + TILE
    cross_at = tiles * step - TILE
    total_rows = cross_at + TILE

    loads = []
    for t in range(tiles):
        cols = pl.ds(t * TILE, TILE)
        loads.append(pltpu.make_async_copy(geno_hbm.at[:, cols], geno.at[:, cols], load_sem.at[t]))
    loads.append(pltpu.make_async_copy(start_hbm, start, load_sem.at[tiles]))
    loads.append(pltpu.make_async_copy(marg_hbm, marg, load_sem.at[tiles + 1]))
    for copy in loads:
        copy.start()

    barrier = pltpu.get_barrier_semaphore()

    @pl.when(has_prev)
    def _():
        pl.semaphore_signal(barrier, inc=1, device_id={"var": prev}, device_id_type=MESH)

    @pl.when(has_next)
    def _():
        pl.semaphore_signal(barrier, inc=1, device_id={"var": following}, device_id_type=MESH)

    for peer in peers:
        pl.semaphore_signal(barrier, inc=1, device_id={"samp": peer}, device_id_type=MESH)
    pl.semaphore_wait(
        barrier, len(peers) + has_prev.astype(jnp.int32) + has_next.astype(jnp.int32)
    )

    geno_copy = pltpu.make_async_remote_copy(
        src_ref=geno_hbm.at[:, pl.ds(last * TILE, TILE)], dst_ref=halo,
        send_sem=geno_sem.at[0], recv_sem=geno_sem.at[1],
        device_id={"var": following}, device_id_type=MESH,
    )

    @pl.when(has_next)
    def _():
        geno_copy.start()

    def part_copy(k, message):
        if message == tiles + 1:
            src, dst = diag, diag_got.at[k]
        else:
            begin = message * step if message < tiles else cross_at
            rows = pl.ds(begin, TILE if message == tiles else HALF if message == last else step)
            src, dst = code.at[rows], got.at[k, rows]
        return pltpu.make_async_remote_copy(
            src_ref=src, dst_ref=dst,
            send_sem=part_send.at[k, message], recv_sem=part_recv.at[k, message],
            device_id={"samp": peers[k]}, device_id_type=MESH,
        )

    def send_part(message):
        for k in range(len(peers)):
            part_copy(k, message).start()

    diag[...] = jnp.zeros_like(diag)
    row, col = iota_pair(TILE)
    on_diagonal = row == col

    for t in range(tiles):
        if t == 0:
            loads[0].wait()
        if t + 1 < tiles:
            loads[t + 1].wait()
        width = min(2, tiles - t) * TILE
        product = gram(geno[:, t * TILE : (t + 1) * TILE], geno[:, t * TILE : t * TILE + width])
        product = product * (inv_total * LD_SCALE)
        block = product[:, :TILE]
        diag[pl.ds(t, 1), :] = jnp.sum(jnp.where(on_diagonal, block, 0.0), axis=0, keepdims=True)
        begin = t * step
        packed = pack_symmetric(block)
        own[begin : begin + HALF] = packed
        code[begin : begin + HALF] = encode(packed)
        if t + 1 < tiles:
            beside = product[:, TILE:]
            own[begin + HALF : begin + step] = beside
            code[begin + HALF : begin + step] = encode(beside)
        send_part(t)
    send_part(tiles + 1)

    loads[tiles].wait()
    loads[tiles + 1].wait()

    def place(sweep, slot, value):
        high, low = split(value)
        eff_hi[sweep, slot * TILE : (slot + 1) * TILE] = high
        eff_lo[sweep, slot * TILE : (slot + 1) * TILE] = low

    def clear(sweep, slot):
        zero = jnp.zeros((TILE, eff_hi.shape[2]), BF16)
        eff_hi[sweep, slot * TILE : (slot + 1) * TILE] = zero
        eff_lo[sweep, slot * TILE : (slot + 1) * TILE] = zero

    for t in range(tiles):
        place(0, t + 1, start[t * TILE : (t + 1) * TILE])
    edge_code[0, 0] = encode(start[:TILE])
    edge_code[0, 1] = encode(start[last * TILE :])

    def edge_copy(sweep, side):
        return pltpu.make_async_remote_copy(
            src_ref=edge_code.at[sweep, side], dst_ref=edge_got.at[sweep, side],
            send_sem=edge_send.at[sweep, side], recv_sem=edge_recv.at[sweep, side],
            device_id={"var": following if side else prev}, device_id_type=MESH,
        )

    def send_edge(sweep, side):
        @pl.when(has_next if side else has_prev)
        def _():
            edge_copy(sweep, side).start()

    def take_edge(sweep, side):
        slot = 0 if side else tiles + 1
        exists = has_prev if side else has_next

        @pl.when(exists)
        def _():
            edge_copy(sweep, side).wait_recv()
            place(sweep, slot, decode(edge_got[sweep, side]))

        @pl.when(jnp.logical_not(exists))
        def _():
            clear(sweep, slot)

    @pl.when(has_prev)
    def _():
        geno_copy.wait_recv()
        product = gram(halo[...], geno[:, :TILE]) * (inv_total * LD_SCALE)
        own[cross_at:total_rows] = product
        code[cross_at:total_rows] = encode(product)
        send_part(tiles)

    send_edge(0, 1)
    send_edge(0, 0)

    def summed(begin, size):
        value = own[begin : begin + size]
        for k in range(len(peers)):
            value = value + decode(got[k, begin : begin + size])
        return value

    def put(tile, slot, value):
        high, low = split(value)
        band_hi[tile, :, slot * TILE : (slot + 1) * TILE] = high
        band_lo[tile, :, slot * TILE : (slot + 1) * TILE] = low

    for k in range(len(peers)):
        part_copy(k, tiles + 1).wait_recv()
    for t in range(tiles):
        for k in range(len(peers)):
            part_copy(k, t).wait_recv()
        begin = t * step
        put(t, 1, unpack_symmetric(summed(begin, HALF)) * (1.0 / LD_SCALE))
        if t + 1 < tiles:
            beside = summed(begin + HALF, TILE) * (1.0 / LD_SCALE)
            put(t, 2, beside)
            put(t + 1, 0, beside.T)

    keep = []
    for t in range(tiles):
        whole = diag[pl.ds(t, 1), :]
        for k in range(len(peers)):
            whole = whole + diag_got[k, pl.ds(t, 1), :]
        column = jnp.sum(jnp.where(on_diagonal, whole, 0.0), axis=1, keepdims=True) * (1.0 / LD_SCALE)
        keep.append(1.0 / ((1.0 - shrinkage) * column + shrinkage))
    limit = limit_ref[...]

    def applied(sweep, tile, first, count):
        cols = slice(first * TILE, (first + count) * TILE)
        rows = slice((tile + first) * TILE, (tile + first + count) * TILE)
        high, low = band_hi[tile, :, cols], band_lo[tile, :, cols]
        near, rest = eff_hi[sweep, rows], eff_lo[sweep, rows]
        dot = functools.partial(jnp.dot, preferred_element_type=F32)
        return dot(high, near) + (dot(high, rest) + dot(low, near))

    def finish(tile, combined):
        adjusted = marg[tile * TILE : (tile + 1) * TILE] - (1.0 - shrinkage) * combined
        shrunk = adjusted - jnp.clip(adjusted, -limit, limit)
        return shrunk * keep[tile]

    for t in range(1, tiles - 1):
        place(1, t + 1, finish(t, applied(0, t, 0, 3)))

    def back_copy():
        return pltpu.make_async_remote_copy(
            src_ref=cross_code, dst_ref=cross_got,
            send_sem=cross_sem.at[0], recv_sem=cross_sem.at[1],
            device_id={"var": prev}, device_id_type=MESH,
        )

    @pl.when(has_prev)
    def _():
        for k in range(len(peers)):
            part_copy(k, tiles).wait_recv()
        crossing = summed(cross_at, TILE)
        cross_code[...] = encode(crossing)
        back_copy().start()
        put(0, 0, crossing.T * (1.0 / LD_SCALE))

    @pl.when(jnp.logical_not(has_prev))
    def _():
        put(0, 0, jnp.zeros((TILE, TILE), F32))

    take_edge(0, 1)
    value = finish(0, applied(0, 0, 0, 3))
    edge_code[1, 0] = encode(value)
    send_edge(1, 0)
    place(1, 1, value)

    @pl.when(has_next)
    def _():
        back_copy().wait_recv()
        put(last, 2, decode(cross_got[...]) * (1.0 / LD_SCALE))

    @pl.when(jnp.logical_not(has_next))
    def _():
        put(last, 2, jnp.zeros((TILE, TILE), F32))

    take_edge(0, 0)
    value = finish(last, applied(0, last, 0, 3))
    edge_code[1, 1] = encode(value)
    send_edge(1, 1)
    place(1, tiles, value)

    stores = []

    def emit(tile, combined):
        rows = pl.ds(tile * TILE, TILE)
        result[tile * TILE : (tile + 1) * TILE] = finish(tile, combined)
        copy = pltpu.make_async_copy(result.at[rows], out_hbm.at[rows], store_sem.at[tile])
        copy.start()
        stores.append(copy)

    for t in range(1, tiles - 1):
        emit(t, applied(1, t, 0, 3))
    part = applied(1, last, 0, 2)
    other = applied(1, 0, 1, 2)
    take_edge(1, 0)
    emit(last, part + applied(1, last, 2, 1))
    take_edge(1, 1)
    emit(0, other + applied(1, 0, 0, 1))

    for copy in stores:
        copy.wait()
    for k in range(len(peers)):
        for message in list(range(tiles)) + [tiles + 1]:
            part_copy(k, message).wait_send()

    @pl.when(has_prev)
    def _():
        for k in range(len(peers)):
            part_copy(k, tiles).wait_send()
        back_copy().wait_send()
        for sweep in range(SWEEPS):
            edge_copy(sweep, 0).wait_send()

    @pl.when(has_next)
    def _():
        geno_copy.wait_send()
        for sweep in range(SWEEPS):
            edge_copy(sweep, 1).wait_send()


def local(genotypes, marginal, start_effects, thresholds):
    samples, variants = genotypes.shape
    traits = marginal.shape[1]
    tiles = variants // TILE
    var_size, samp_size = lax.axis_size("var"), lax.axis_size("samp")
    others = samp_size - 1
    rows = tiles * (HALF + TILE)
    dma = pltpu.SemaphoreType.DMA
    body = functools.partial(
        kernel, tiles, var_size, samp_size, 1.0 / (samples * samp_size)
    )
    return pl.pallas_call(
        body,
        out_shape=jax.ShapeDtypeStruct((variants, traits), F32),
        in_specs=[pl.BlockSpec(memory_space=pl.ANY)] * 3 + [pl.BlockSpec(memory_space=pltpu.VMEM)],
        out_specs=pl.BlockSpec(memory_space=pl.ANY),
        scratch_shapes=[
            pltpu.VMEM((samples, variants), BF16),
            pltpu.VMEM((samples, TILE), BF16),
            pltpu.VMEM((variants, traits), F32),
            pltpu.VMEM((variants, traits), F32),
            pltpu.VMEM((rows, TILE), F32),
            pltpu.VMEM((rows, TILE), BF16),
            pltpu.VMEM((others, rows, TILE), BF16),
            pltpu.VMEM((8, TILE), F32),
            pltpu.VMEM((others, 8, TILE), F32),
            pltpu.VMEM((tiles, TILE, 3 * TILE), BF16),
            pltpu.VMEM((tiles, TILE, 3 * TILE), BF16),
            pltpu.VMEM((SWEEPS, (tiles + 2) * TILE, traits), BF16),
            pltpu.VMEM((SWEEPS, (tiles + 2) * TILE, traits), BF16),
            pltpu.VMEM((SWEEPS, 2, TILE, traits), BF16),
            pltpu.VMEM((SWEEPS, 2, TILE, traits), BF16),
            pltpu.VMEM((TILE, TILE), BF16),
            pltpu.VMEM((TILE, TILE), BF16),
            pltpu.VMEM((variants, traits), F32),
            dma((tiles + 2,)),
            dma((tiles,)),
            dma((2,)),
            dma((others, tiles + 2)),
            dma((others, tiles + 2)),
            dma((2,)),
            dma((SWEEPS, 2)),
            dma((SWEEPS, 2)),
        ],
        compiler_params=pltpu.CompilerParams(
            collective_id=0, has_side_effects=True, vmem_limit_bytes=60 * 1024 * 1024
        ),
    )(genotypes, marginal, start_effects, thresholds[None, :])


def solution(mesh):
    in_specs = (P("samp", "var"), P("var", "samp"), P("var", "samp"), P("samp"))
    out_specs = P("var", "samp")
    return jax.shard_map(local, mesh=mesh, in_specs=in_specs, out_specs=out_specs, check_vma=False)
```

```python
import functools

import jax
import jax.numpy as jnp
from jax import lax
from jax.experimental import pallas as pl
from jax.experimental.pallas import tpu as pltpu
from jax.sharding import PartitionSpec as P

TILE = 256
HALF = TILE // 2
SWEEPS = 2
CHUNKS = 4
VMEM_BYTES = 40 * 1024 * 1024
LD_SCALE = 1024.0

shrinkage = 0.2
MESH = pl.DeviceIdType.MESH
F32 = jnp.float32
BF16 = jnp.bfloat16


def encode(value):
    square = value * value
    fourth = square * square
    eighth = fourth * fourth
    return jnp.where(value < 0, -eighth, eighth).astype(BF16)


def decode(code):
    code = code.astype(F32)
    root = jnp.sqrt(jnp.sqrt(jnp.sqrt(jnp.abs(code))))
    return jnp.where(code < 0, -root, root)


def split(value):
    high = value.astype(BF16)
    return high, (value - high.astype(F32)).astype(BF16)


def iota_pair(size):
    row = lax.broadcasted_iota(jnp.int32, (size, size), 0)
    col = lax.broadcasted_iota(jnp.int32, (size, size), 1)
    return row, col


def pack_symmetric(tile):
    row, col = iota_pair(HALF)
    mixed = jnp.where(row < col, tile[:HALF, :HALF], tile[HALF:, HALF:])
    return jnp.concatenate([mixed, tile[:HALF, HALF:]], axis=1)


def unpack_symmetric(packed):
    row, col = iota_pair(HALF)
    mixed, corner = packed[:, :HALF], packed[:, HALF:]
    upper = jnp.where(row < col, mixed, 0.0)
    lower = jnp.where(row > col, mixed, 0.0)
    first = jnp.concatenate([upper + upper.T, corner], axis=1)
    second = jnp.concatenate([corner.T, lower + lower.T], axis=1)
    return jnp.concatenate([first, second], axis=0)


def gram(left, right):
    return lax.dot_general(left, right, (((0,), (0,)), ((), ())), preferred_element_type=F32)


def kernel(
    tiles, var_size, samp_size, inv_total,
    geno_hbm, marg_hbm, start_hbm, limit_hbm, out,
    geno, halo, marg, start, limit_row, own, code, got, diag, diag_got,
    band_hi, band_lo, eff_hi, eff_lo, edge_code, edge_got, cross_code, cross_got,
    load_sem, geno_send, geno_recv, part_send, part_recv, cross_sem, edge_send, edge_recv,
):
    var = lax.axis_index("var")
    samp = lax.axis_index("samp")
    has_prev = var > 0
    has_next = var < var_size - 1
    prev, following = var - 1, var + 1
    peers = [lax.rem(samp + k, samp_size) for k in range(1, samp_size)]
    last = tiles - 1
    pieces, width = edge_code.shape[2], edge_code.shape[4]
    slices = [slice(c * width, (c + 1) * width) for c in range(pieces)]

    step = HALF + TILE
    cross_at = tiles * step - TILE
    total_rows = cross_at + TILE

    loads = []
    for t in range(tiles):
        cols = pl.ds(t * TILE, TILE)
        loads.append(pltpu.make_async_copy(geno_hbm.at[:, cols], geno.at[:, cols], load_sem.at[t]))
    loads.append(pltpu.make_async_copy(start_hbm, start, load_sem.at[tiles]))
    loads.append(pltpu.make_async_copy(marg_hbm, marg, load_sem.at[tiles + 1]))
    loads.append(pltpu.make_async_copy(limit_hbm, limit_row, load_sem.at[tiles + 2]))
    for copy in loads:
        copy.start()

    barrier = pltpu.get_barrier_semaphore()

    @pl.when(has_prev)
    def _():
        pl.semaphore_signal(barrier, inc=1, device_id={"var": prev}, device_id_type=MESH)

    @pl.when(has_next)
    def _():
        pl.semaphore_signal(barrier, inc=1, device_id={"var": following}, device_id_type=MESH)

    for peer in peers:
        pl.semaphore_signal(barrier, inc=1, device_id={"samp": peer}, device_id_type=MESH)
    pl.semaphore_wait(
        barrier, len(peers) + has_prev.astype(jnp.int32) + has_next.astype(jnp.int32)
    )

    depth = geno.shape[0] // CHUNKS

    def geno_copy(chunk):
        rows = pl.ds(chunk * depth, depth)
        return pltpu.make_async_remote_copy(
            src_ref=geno_hbm.at[rows, pl.ds(last * TILE, TILE)], dst_ref=halo.at[rows],
            send_sem=geno_send.at[chunk], recv_sem=geno_recv.at[chunk],
            device_id={"var": following}, device_id_type=MESH,
        )

    @pl.when(has_next)
    def _():
        for chunk in range(CHUNKS):
            geno_copy(chunk).start()

    def part_copy(k, message):
        if message == tiles + 1:
            src, dst = diag, diag_got.at[k]
        else:
            begin = message * step if message < tiles else cross_at
            rows = pl.ds(begin, TILE if message == tiles else HALF if message == last else step)
            src, dst = code.at[rows], got.at[k, rows]
        return pltpu.make_async_remote_copy(
            src_ref=src, dst_ref=dst,
            send_sem=part_send.at[k, message], recv_sem=part_recv.at[k, message],
            device_id={"samp": peers[k]}, device_id_type=MESH,
        )

    def send_part(message):
        for k in range(len(peers)):
            part_copy(k, message).start()

    diag[...] = jnp.zeros_like(diag)
    row, col = iota_pair(TILE)
    on_diagonal = row == col

    for t in range(tiles):
        if t == 0:
            loads[0].wait()
        if t + 1 < tiles:
            loads[t + 1].wait()
        reach = min(t + 2, tiles) * TILE
        product = gram(geno[:, t * TILE : (t + 1) * TILE], geno[:, t * TILE : reach])
        product = product * (inv_total * LD_SCALE)
        block = product[:, :TILE]
        diag[pl.ds(t, 1), :] = jnp.sum(jnp.where(on_diagonal, block, 0.0), axis=0, keepdims=True)
        begin = t * step
        packed = pack_symmetric(block)
        own[begin : begin + HALF] = packed
        code[begin : begin + HALF] = encode(packed)
        if t + 1 < tiles:
            beside = product[:, TILE:]
            own[begin + HALF : begin + step] = beside
            code[begin + HALF : begin + step] = encode(beside)
        send_part(t)
    send_part(tiles + 1)

    for copy in loads[tiles:]:
        copy.wait()
    everything = slice(0, pieces * width)

    def place(sweep, slot, value, cols=everything):
        high, low = split(value)
        eff_hi[sweep, slot * TILE : (slot + 1) * TILE, cols] = high
        eff_lo[sweep, slot * TILE : (slot + 1) * TILE, cols] = low

    def edge_copy(sweep, side, piece):
        return pltpu.make_async_remote_copy(
            src_ref=edge_code.at[sweep, side, piece], dst_ref=edge_got.at[sweep, side, piece],
            send_sem=edge_send.at[sweep, side, piece], recv_sem=edge_recv.at[sweep, side, piece],
            device_id={"var": following if side else prev}, device_id_type=MESH,
        )

    def send_edge(sweep, side, piece):
        @pl.when(has_next if side else has_prev)
        def _():
            edge_copy(sweep, side, piece).start()

    def take_edge(sweep, side, piece):
        slot = 0 if side else tiles + 1
        exists = has_prev if side else has_next

        @pl.when(exists)
        def _():
            edge_copy(sweep, side, piece).wait_recv()
            place(sweep, slot, decode(edge_got[sweep, side, piece]), slices[piece])

        @pl.when(jnp.logical_not(exists))
        def _():
            place(sweep, slot, jnp.zeros((TILE, width), F32), slices[piece])

    for side, rows in ((1, slice(last * TILE, tiles * TILE)), (0, slice(0, TILE))):
        for piece in range(pieces):
            edge_code[0, side, piece] = encode(start[rows, slices[piece]])
            if side:
                send_edge(0, side, piece)
    for t in range(tiles):
        place(0, t + 1, start[t * TILE : (t + 1) * TILE])

    @pl.when(has_prev)
    def _():
        crossing = jnp.zeros((TILE, TILE), F32)
        for chunk in range(CHUNKS):
            rows = slice(chunk * depth, (chunk + 1) * depth)
            geno_copy(chunk).wait_recv()
            if chunk == CHUNKS - 1:
                for piece in range(pieces):
                    edge_copy(0, 0, piece).start()
            crossing = crossing + gram(halo[rows], geno[rows, :TILE])
        crossing = crossing * (inv_total * LD_SCALE)
        own[cross_at:total_rows] = crossing
        code[cross_at:total_rows] = encode(crossing)
        send_part(tiles)

    def summed(begin, size):
        value = own[begin : begin + size]
        for k in range(len(peers)):
            value = value + decode(got[k, begin : begin + size])
        return value

    def put(tile, slot, value):
        high, low = split(value)
        band_hi[tile, :, slot * TILE : (slot + 1) * TILE] = high
        band_lo[tile, :, slot * TILE : (slot + 1) * TILE] = low

    for k in range(len(peers)):
        part_copy(k, tiles + 1).wait_recv()
    for t in range(tiles):
        for k in range(len(peers)):
            part_copy(k, t).wait_recv()
        begin = t * step
        put(t, 1, unpack_symmetric(summed(begin, HALF)) * (1.0 / LD_SCALE))
        if t + 1 < tiles:
            beside = summed(begin + HALF, TILE) * (1.0 / LD_SCALE)
            put(t, 2, beside)
            put(t + 1, 0, beside.T)

    keep = []
    for t in range(tiles):
        whole = diag[pl.ds(t, 1), :]
        for k in range(len(peers)):
            whole = whole + diag_got[k, pl.ds(t, 1), :]
        column = jnp.sum(jnp.where(on_diagonal, whole, 0.0), axis=1, keepdims=True) * (1.0 / LD_SCALE)
        keep.append(1.0 / ((1.0 - shrinkage) * column + shrinkage))
    limit = limit_row[...]

    def applied(sweep, tile, first, count, cols=everything):
        across = slice(first * TILE, (first + count) * TILE)
        rows = slice((tile + first) * TILE, (tile + first + count) * TILE)
        high, low = band_hi[tile, :, across], band_lo[tile, :, across]
        near, rest = eff_hi[sweep, rows, cols], eff_lo[sweep, rows, cols]
        dot = functools.partial(jnp.dot, preferred_element_type=F32)
        return dot(high, near) + (dot(high, rest) + dot(low, near))

    def finish(tile, combined, cols=everything):
        adjusted = marg[tile * TILE : (tile + 1) * TILE, cols] - (1.0 - shrinkage) * combined
        bound = limit[:, cols]
        return (adjusted - jnp.clip(adjusted, -bound, bound)) * keep[tile]

    for t in range(1, tiles - 1):
        place(1, t + 1, finish(t, applied(0, t, 0, 3)))
    near_first = applied(0, 0, 1, 2)
    near_last = applied(0, last, 0, 2)

    def back_copy():
        return pltpu.make_async_remote_copy(
            src_ref=cross_code, dst_ref=cross_got,
            send_sem=cross_sem.at[0], recv_sem=cross_sem.at[1],
            device_id={"var": prev}, device_id_type=MESH,
        )

    @pl.when(has_prev)
    def _():
        for k in range(len(peers)):
            part_copy(k, tiles).wait_recv()
        crossing = summed(cross_at, TILE)
        cross_code[...] = encode(crossing)
        back_copy().start()
        put(0, 0, crossing.T * (1.0 / LD_SCALE))

    @pl.when(jnp.logical_not(has_prev))
    def _():
        put(0, 0, jnp.zeros((TILE, TILE), F32))

    for piece, cols in enumerate(slices):
        take_edge(0, 1, piece)
        value = finish(0, near_first[:, cols] + applied(0, 0, 0, 1, cols), cols)
        edge_code[1, 0, piece] = encode(value)
        send_edge(1, 0, piece)
        place(1, 1, value, cols)

    for piece in range(pieces):
        take_edge(0, 0, piece)

    @pl.when(has_next)
    def _():
        back_copy().wait_recv()
        put(last, 2, decode(cross_got[...]) * (1.0 / LD_SCALE))

    @pl.when(jnp.logical_not(has_next))
    def _():
        put(last, 2, jnp.zeros((TILE, TILE), F32))

    for piece, cols in enumerate(slices):
        value = finish(last, near_last[:, cols] + applied(0, last, 2, 1, cols), cols)
        edge_code[1, 1, piece] = encode(value)
        send_edge(1, 1, piece)
        place(1, tiles, value, cols)

    for t in range(1, tiles - 1):
        out[t * TILE : (t + 1) * TILE] = finish(t, applied(1, t, 0, 3))
    near_last = applied(1, last, 0, 2)
    near_first = applied(1, 0, 1, 2)
    for piece, cols in enumerate(slices):
        take_edge(1, 0, piece)
        combined = near_last[:, cols] + applied(1, last, 2, 1, cols)
        out[last * TILE : tiles * TILE, cols] = finish(last, combined, cols)
    for piece, cols in enumerate(slices):
        take_edge(1, 1, piece)
        combined = near_first[:, cols] + applied(1, 0, 0, 1, cols)
        out[:TILE, cols] = finish(0, combined, cols)

    for k in range(len(peers)):
        for message in list(range(tiles)) + [tiles + 1]:
            part_copy(k, message).wait_send()

    @pl.when(has_prev)
    def _():
        for k in range(len(peers)):
            part_copy(k, tiles).wait_send()
        back_copy().wait_send()
        for sweep in range(SWEEPS):
            for piece in range(pieces):
                edge_copy(sweep, 0, piece).wait_send()

    @pl.when(has_next)
    def _():
        for chunk in range(CHUNKS):
            geno_copy(chunk).wait_send()
        for sweep in range(SWEEPS):
            for piece in range(pieces):
                edge_copy(sweep, 1, piece).wait_send()


def local(genotypes, marginal, start_effects, thresholds):
    samples, variants = genotypes.shape
    traits = marginal.shape[1]
    tiles = variants // TILE
    var_size, samp_size = lax.axis_size("var"), lax.axis_size("samp")
    others = samp_size - 1
    rows = tiles * (HALF + TILE)
    pieces = 2 if traits % 256 == 0 else 1
    width = traits // pieces
    dma = pltpu.SemaphoreType.DMA
    body = functools.partial(
        kernel, tiles, var_size, samp_size, 1.0 / (samples * samp_size)
    )
    return pl.pallas_call(
        body,
        out_shape=jax.ShapeDtypeStruct((variants, traits), F32),
        in_specs=[pl.BlockSpec(memory_space=pltpu.HBM)] * 4,
        out_specs=pl.BlockSpec(memory_space=pltpu.VMEM),
        scratch_shapes=[
            pltpu.VMEM((samples, variants), BF16),
            pltpu.VMEM((samples, TILE), BF16),
            pltpu.VMEM((variants, traits), F32),
            pltpu.VMEM((variants, traits), F32),
            pltpu.VMEM((1, traits), F32),
            pltpu.VMEM((rows, TILE), F32),
            pltpu.VMEM((rows, TILE), BF16),
            pltpu.VMEM((others, rows, TILE), BF16),
            pltpu.VMEM((8, TILE), F32),
            pltpu.VMEM((others, 8, TILE), F32),
            pltpu.VMEM((tiles, TILE, 3 * TILE), BF16),
            pltpu.VMEM((tiles, TILE, 3 * TILE), BF16),
            pltpu.VMEM((SWEEPS, (tiles + 2) * TILE, traits), BF16),
            pltpu.VMEM((SWEEPS, (tiles + 2) * TILE, traits), BF16),
            pltpu.VMEM((SWEEPS, 2, pieces, TILE, width), BF16),
            pltpu.VMEM((SWEEPS, 2, pieces, TILE, width), BF16),
            pltpu.VMEM((TILE, TILE), BF16),
            pltpu.VMEM((TILE, TILE), BF16),
            dma((tiles + 3,)),
            dma((CHUNKS,)),
            dma((CHUNKS,)),
            dma((others, tiles + 2)),
            dma((others, tiles + 2)),
            dma((2,)),
            dma((SWEEPS, 2, pieces)),
            dma((SWEEPS, 2, pieces)),
        ],
        compiler_params=pltpu.CompilerParams(
            collective_id=0, has_side_effects=True, vmem_limit_bytes=VMEM_BYTES
        ),
    )(*(
        pltpu.with_memory_space_constraint(array, pltpu.HBM)
        for array in (genotypes, marginal, start_effects, thresholds[None, :])
    ))


def solution(mesh):
    in_specs = (P("samp", "var"), P("var", "samp"), P("var", "samp"), P("samp"))
    out_specs = P("var", "samp")
    return jax.shard_map(local, mesh=mesh, in_specs=in_specs, out_specs=out_specs, check_vma=False)
```

```python
import functools

import jax
import jax.numpy as jnp
from jax import lax
from jax.experimental import pallas as pl
from jax.experimental.pallas import tpu as pltpu
from jax.sharding import PartitionSpec as P

TILE = 256
HALF = TILE // 2
SWEEPS = 2
CHUNKS = 4
TINY = 2.0**-126
VMEM_BYTES = 40 * 1024 * 1024
LD_SCALE = 1024.0

shrinkage = 0.2
MESH = pl.DeviceIdType.MESH
F32 = jnp.float32
BF16 = jnp.bfloat16


def encode(value):
    square = value * value
    fourth = square * square
    eighth = fourth * fourth
    return jnp.where(value < 0, -eighth, eighth).astype(BF16)


def decode(code):
    code = code.astype(F32)
    size = jnp.abs(code)
    fourth_root = lax.rsqrt(lax.rsqrt(jnp.maximum(size, TINY)))
    root = jnp.where(size < TINY, 0.0, fourth_root * lax.rsqrt(fourth_root))
    return jnp.where(code < 0, -root, root)


def split(value):
    high = value.astype(BF16)
    return high, (value - high.astype(F32)).astype(BF16)


def iota_pair(size):
    row = lax.broadcasted_iota(jnp.int32, (size, size), 0)
    col = lax.broadcasted_iota(jnp.int32, (size, size), 1)
    return row, col


def pack_symmetric(tile):
    row, col = iota_pair(HALF)
    mixed = jnp.where(row < col, tile[:HALF, :HALF], tile[HALF:, HALF:])
    return jnp.concatenate([mixed, tile[:HALF, HALF:]], axis=1)


def unpack_symmetric(packed):
    row, col = iota_pair(HALF)
    mixed, corner = packed[:, :HALF], packed[:, HALF:]
    upper = jnp.where(row < col, mixed, 0.0)
    lower = jnp.where(row > col, mixed, 0.0)
    first = jnp.concatenate([upper + upper.T, corner], axis=1)
    second = jnp.concatenate([corner.T, lower + lower.T], axis=1)
    return jnp.concatenate([first, second], axis=0)


def gram(left, right):
    return lax.dot_general(left, right, (((0,), (0,)), ((), ())), preferred_element_type=F32)


def kernel(
    tiles, var_size, samp_size, inv_total,
    geno_hbm, marg_hbm, start_hbm, limit_hbm, out,
    geno, halo, marg, start, limit_row, own, code, got, diag, diag_got,
    band_hi, band_lo, eff_hi, eff_lo, edge_code, edge_got, cross_code, cross_got,
    load_sem, geno_send, geno_recv, part_send, part_recv, cross_sem, edge_send, edge_recv,
):
    var = lax.axis_index("var")
    samp = lax.axis_index("samp")
    has_prev = var > 0
    has_next = var < var_size - 1
    prev, following = var - 1, var + 1
    peers = [lax.rem(samp + k, samp_size) for k in range(1, samp_size)]
    last = tiles - 1
    pieces, width = edge_code.shape[2], edge_code.shape[4]
    slices = [slice(c * width, (c + 1) * width) for c in range(pieces)]

    step = HALF + TILE
    cross_at = tiles * step - TILE
    total_rows = cross_at + TILE

    loads = []
    for t in range(tiles):
        cols = pl.ds(t * TILE, TILE)
        loads.append(pltpu.make_async_copy(geno_hbm.at[:, cols], geno.at[:, cols], load_sem.at[t]))
    loads.append(pltpu.make_async_copy(start_hbm, start, load_sem.at[tiles]))
    loads.append(pltpu.make_async_copy(marg_hbm, marg, load_sem.at[tiles + 1]))
    loads.append(pltpu.make_async_copy(limit_hbm, limit_row, load_sem.at[tiles + 2]))
    for copy in loads:
        copy.start()

    barrier = pltpu.get_barrier_semaphore()

    @pl.when(has_prev)
    def _():
        pl.semaphore_signal(barrier, inc=1, device_id={"var": prev}, device_id_type=MESH)

    @pl.when(has_next)
    def _():
        pl.semaphore_signal(barrier, inc=1, device_id={"var": following}, device_id_type=MESH)

    for peer in peers:
        pl.semaphore_signal(barrier, inc=1, device_id={"samp": peer}, device_id_type=MESH)
    pl.semaphore_wait(
        barrier, len(peers) + has_prev.astype(jnp.int32) + has_next.astype(jnp.int32)
    )

    depth = geno.shape[0] // CHUNKS

    def geno_copy(chunk):
        rows = pl.ds(chunk * depth, depth)
        return pltpu.make_async_remote_copy(
            src_ref=geno_hbm.at[rows, pl.ds(last * TILE, TILE)], dst_ref=halo.at[rows],
            send_sem=geno_send.at[chunk], recv_sem=geno_recv.at[chunk],
            device_id={"var": following}, device_id_type=MESH,
        )

    @pl.when(has_next)
    def _():
        for chunk in range(CHUNKS):
            geno_copy(chunk).start()

    def part_copy(k, message):
        if message == tiles + 1:
            src, dst = diag, diag_got.at[k]
        else:
            begin = message * step if message < tiles else cross_at
            rows = pl.ds(begin, TILE if message == tiles else HALF if message == last else step)
            src, dst = code.at[rows], got.at[k, rows]
        return pltpu.make_async_remote_copy(
            src_ref=src, dst_ref=dst,
            send_sem=part_send.at[k, message], recv_sem=part_recv.at[k, message],
            device_id={"samp": peers[k]}, device_id_type=MESH,
        )

    def send_part(message):
        for k in range(len(peers)):
            part_copy(k, message).start()

    diag[...] = jnp.zeros_like(diag)
    row, col = iota_pair(TILE)
    on_diagonal = row == col

    for t in range(tiles):
        if t == 0:
            loads[0].wait()
        if t + 1 < tiles:
            loads[t + 1].wait()
        reach = min(t + 2, tiles) * TILE
        product = gram(geno[:, t * TILE : (t + 1) * TILE], geno[:, t * TILE : reach])
        product = product * (inv_total * LD_SCALE)
        block = product[:, :TILE]
        diag[pl.ds(t, 1), :] = jnp.sum(jnp.where(on_diagonal, block, 0.0), axis=0, keepdims=True)
        begin = t * step
        packed = pack_symmetric(block)
        own[begin : begin + HALF] = packed
        code[begin : begin + HALF] = encode(packed)
        if t + 1 < tiles:
            beside = product[:, TILE:]
            own[begin + HALF : begin + step] = beside
            code[begin + HALF : begin + step] = encode(beside)
        if t == last:
            send_part(tiles + 1)
        send_part(t)

    for copy in loads[tiles:]:
        copy.wait()
    everything = slice(0, pieces * width)

    def place(sweep, slot, value, cols=everything):
        high, low = split(value)
        eff_hi[sweep, slot * TILE : (slot + 1) * TILE, cols] = high
        eff_lo[sweep, slot * TILE : (slot + 1) * TILE, cols] = low

    def edge_copy(sweep, side, piece):
        return pltpu.make_async_remote_copy(
            src_ref=edge_code.at[sweep, side, piece], dst_ref=edge_got.at[sweep, side, piece],
            send_sem=edge_send.at[sweep, side, piece], recv_sem=edge_recv.at[sweep, side, piece],
            device_id={"var": following if side else prev}, device_id_type=MESH,
        )

    def send_edge(sweep, side, piece):
        @pl.when(has_next if side else has_prev)
        def _():
            edge_copy(sweep, side, piece).start()

    def take_edge(sweep, side, piece):
        slot = 0 if side else tiles + 1
        exists = has_prev if side else has_next

        @pl.when(exists)
        def _():
            edge_copy(sweep, side, piece).wait_recv()
            place(sweep, slot, decode(edge_got[sweep, side, piece]), slices[piece])

        @pl.when(jnp.logical_not(exists))
        def _():
            place(sweep, slot, jnp.zeros((TILE, width), F32), slices[piece])

    for side, rows in ((1, slice(last * TILE, tiles * TILE)), (0, slice(0, TILE))):
        for piece in range(pieces):
            edge_code[0, side, piece] = encode(start[rows, slices[piece]])
            if side:
                send_edge(0, side, piece)
    for t in range(tiles):
        place(0, t + 1, start[t * TILE : (t + 1) * TILE])

    def summed(begin, size):
        value = own[begin : begin + size]
        for k in range(len(peers)):
            value = value + decode(got[k, begin : begin + size])
        return value

    def put(tile, slot, value):
        high, low = split(value)
        band_hi[tile, :, slot * TILE : (slot + 1) * TILE] = high
        band_lo[tile, :, slot * TILE : (slot + 1) * TILE] = low

    def applied(sweep, tile, first, count, cols=everything):
        across = slice(first * TILE, (first + count) * TILE)
        rows = slice((tile + first) * TILE, (tile + first + count) * TILE)
        high, low = band_hi[tile, :, across], band_lo[tile, :, across]
        near, rest = eff_hi[sweep, rows, cols], eff_lo[sweep, rows, cols]
        dot = functools.partial(jnp.dot, preferred_element_type=F32)
        return dot(high, near) + (dot(high, rest) + dot(low, near))

    def add_tile(t):
        for k in range(len(peers)):
            part_copy(k, t).wait_recv()
        begin = t * step
        put(t, 1, unpack_symmetric(summed(begin, HALF)) * (1.0 / LD_SCALE))
        if t + 1 < tiles:
            beside = summed(begin + HALF, TILE) * (1.0 / LD_SCALE)
            put(t, 2, beside)
            put(t + 1, 0, beside.T)

    for t in range(last):
        add_tile(t)
    near_first = applied(0, 0, 1, 2)

    @pl.when(has_prev)
    def _():
        crossing = jnp.zeros((TILE, TILE), F32)
        for chunk in range(CHUNKS):
            rows = slice(chunk * depth, (chunk + 1) * depth)
            geno_copy(chunk).wait_recv()
            if chunk == CHUNKS - 1:
                for piece in range(pieces):
                    edge_copy(0, 0, piece).start()
            crossing = crossing + gram(halo[rows], geno[rows, :TILE])
        crossing = crossing * (inv_total * LD_SCALE)
        own[cross_at:total_rows] = crossing
        code[cross_at:total_rows] = encode(crossing)
        send_part(tiles)

    add_tile(last)
    for k in range(len(peers)):
        part_copy(k, tiles + 1).wait_recv()
    keep = []
    for t in range(tiles):
        whole = diag[pl.ds(t, 1), :]
        for k in range(len(peers)):
            whole = whole + diag_got[k, pl.ds(t, 1), :]
        column = jnp.sum(jnp.where(on_diagonal, whole, 0.0), axis=1, keepdims=True) * (1.0 / LD_SCALE)
        keep.append(1.0 / ((1.0 - shrinkage) * column + shrinkage))
    limit = limit_row[...]

    def finish(tile, combined, cols=everything):
        adjusted = marg[tile * TILE : (tile + 1) * TILE, cols] - (1.0 - shrinkage) * combined
        bound = limit[:, cols]
        return (adjusted - jnp.clip(adjusted, -bound, bound)) * keep[tile]

    for t in range(1, tiles - 1):
        place(1, t + 1, finish(t, applied(0, t, 0, 3)))
    near_last = applied(0, last, 0, 2)

    def back_copy():
        return pltpu.make_async_remote_copy(
            src_ref=cross_code, dst_ref=cross_got,
            send_sem=cross_sem.at[0], recv_sem=cross_sem.at[1],
            device_id={"var": prev}, device_id_type=MESH,
        )

    @pl.when(has_prev)
    def _():
        for k in range(len(peers)):
            part_copy(k, tiles).wait_recv()
        crossing = summed(cross_at, TILE)
        cross_code[...] = encode(crossing)
        back_copy().start()
        put(0, 0, crossing.T * (1.0 / LD_SCALE))

    @pl.when(jnp.logical_not(has_prev))
    def _():
        put(0, 0, jnp.zeros((TILE, TILE), F32))

    for piece, cols in enumerate(slices):
        take_edge(0, 1, piece)
        value = finish(0, near_first[:, cols] + applied(0, 0, 0, 1, cols), cols)
        edge_code[1, 0, piece] = encode(value)
        send_edge(1, 0, piece)
        place(1, 1, value, cols)

    for piece in range(pieces):
        take_edge(0, 0, piece)

    @pl.when(has_next)
    def _():
        back_copy().wait_recv()
        put(last, 2, decode(cross_got[...]) * (1.0 / LD_SCALE))

    @pl.when(jnp.logical_not(has_next))
    def _():
        put(last, 2, jnp.zeros((TILE, TILE), F32))

    for piece, cols in enumerate(slices):
        value = finish(last, near_last[:, cols] + applied(0, last, 2, 1, cols), cols)
        edge_code[1, 1, piece] = encode(value)
        send_edge(1, 1, piece)
        place(1, tiles, value, cols)

    for t in range(1, tiles - 1):
        out[t * TILE : (t + 1) * TILE] = finish(t, applied(1, t, 0, 3))
    near_last = applied(1, last, 0, 2)
    near_first = applied(1, 0, 1, 2)
    for piece, cols in enumerate(slices):
        take_edge(1, 0, piece)
        combined = near_last[:, cols] + applied(1, last, 2, 1, cols)
        out[last * TILE : tiles * TILE, cols] = finish(last, combined, cols)
    for piece, cols in enumerate(slices):
        take_edge(1, 1, piece)
        combined = near_first[:, cols] + applied(1, 0, 0, 1, cols)
        out[:TILE, cols] = finish(0, combined, cols)

    for k in range(len(peers)):
        for message in list(range(tiles)) + [tiles + 1]:
            part_copy(k, message).wait_send()

    @pl.when(has_prev)
    def _():
        for k in range(len(peers)):
            part_copy(k, tiles).wait_send()
        back_copy().wait_send()
        for sweep in range(SWEEPS):
            for piece in range(pieces):
                edge_copy(sweep, 0, piece).wait_send()

    @pl.when(has_next)
    def _():
        for chunk in range(CHUNKS):
            geno_copy(chunk).wait_send()
        for sweep in range(SWEEPS):
            for piece in range(pieces):
                edge_copy(sweep, 1, piece).wait_send()


def local(genotypes, marginal, start_effects, thresholds):
    samples, variants = genotypes.shape
    traits = marginal.shape[1]
    tiles = variants // TILE
    var_size, samp_size = lax.axis_size("var"), lax.axis_size("samp")
    others = samp_size - 1
    rows = tiles * (HALF + TILE)
    pieces = 2 if traits % 256 == 0 else 1
    width = traits // pieces
    dma = pltpu.SemaphoreType.DMA
    body = functools.partial(
        kernel, tiles, var_size, samp_size, 1.0 / (samples * samp_size)
    )
    return pl.pallas_call(
        body,
        out_shape=jax.ShapeDtypeStruct((variants, traits), F32),
        in_specs=[pl.BlockSpec(memory_space=pltpu.HBM)] * 4,
        out_specs=pl.BlockSpec(memory_space=pltpu.VMEM),
        scratch_shapes=[
            pltpu.VMEM((samples, variants), BF16),
            pltpu.VMEM((samples, TILE), BF16),
            pltpu.VMEM((variants, traits), F32),
            pltpu.VMEM((variants, traits), F32),
            pltpu.VMEM((1, traits), F32),
            pltpu.VMEM((rows, TILE), F32),
            pltpu.VMEM((rows, TILE), BF16),
            pltpu.VMEM((others, rows, TILE), BF16),
            pltpu.VMEM((8, TILE), F32),
            pltpu.VMEM((others, 8, TILE), F32),
            pltpu.VMEM((tiles, TILE, 3 * TILE), BF16),
            pltpu.VMEM((tiles, TILE, 3 * TILE), BF16),
            pltpu.VMEM((SWEEPS, (tiles + 2) * TILE, traits), BF16),
            pltpu.VMEM((SWEEPS, (tiles + 2) * TILE, traits), BF16),
            pltpu.VMEM((SWEEPS, 2, pieces, TILE, width), BF16),
            pltpu.VMEM((SWEEPS, 2, pieces, TILE, width), BF16),
            pltpu.VMEM((TILE, TILE), BF16),
            pltpu.VMEM((TILE, TILE), BF16),
            dma((tiles + 3,)),
            dma((CHUNKS,)),
            dma((CHUNKS,)),
            dma((others, tiles + 2)),
            dma((others, tiles + 2)),
            dma((2,)),
            dma((SWEEPS, 2, pieces)),
            dma((SWEEPS, 2, pieces)),
        ],
        compiler_params=pltpu.CompilerParams(
            collective_id=0, has_side_effects=True, vmem_limit_bytes=VMEM_BYTES
        ),
    )(*(
        pltpu.with_memory_space_constraint(array, pltpu.HBM)
        for array in (genotypes, marginal, start_effects, thresholds[None, :])
    ))


def solution(mesh):
    in_specs = (P("samp", "var"), P("var", "samp"), P("var", "samp"), P("samp"))
    out_specs = P("var", "samp")
    return jax.shard_map(local, mesh=mesh, in_specs=in_specs, out_specs=out_specs, check_vma=False)
```

```python
import functools

import jax
import jax.numpy as jnp
from jax import lax
from jax.experimental import pallas as pl
from jax.experimental.pallas import tpu as pltpu
from jax.sharding import PartitionSpec as P

TILE = 256
HALF = TILE // 2
SWEEPS = 2
CHUNKS = 4
TINY = 2.0**-126
VMEM_BYTES = 40 * 1024 * 1024
LD_SCALE = 1024.0

shrinkage = 0.2
MESH = pl.DeviceIdType.MESH
F32 = jnp.float32
BF16 = jnp.bfloat16


def encode(value):
    square = value * value
    fourth = square * square
    eighth = fourth * fourth
    return jnp.where(value < 0, -eighth, eighth).astype(BF16)


def decode(code):
    code = code.astype(F32)
    size = jnp.abs(code)
    fourth_root = lax.rsqrt(lax.rsqrt(jnp.maximum(size, TINY)))
    root = jnp.where(size < TINY, 0.0, fourth_root * lax.rsqrt(fourth_root))
    return jnp.where(code < 0, -root, root)


def split(value):
    high = value.astype(BF16)
    return high, (value - high.astype(F32)).astype(BF16)


def iota_pair(size):
    row = lax.broadcasted_iota(jnp.int32, (size, size), 0)
    col = lax.broadcasted_iota(jnp.int32, (size, size), 1)
    return row, col


def pack_symmetric(tile):
    row, col = iota_pair(HALF)
    mixed = jnp.where(row < col, tile[:HALF, :HALF], tile[HALF:, HALF:])
    return jnp.concatenate([mixed, tile[:HALF, HALF:]], axis=1)


def unpack_symmetric(packed):
    row, col = iota_pair(HALF)
    mixed, corner = packed[:, :HALF], packed[:, HALF:]
    upper = jnp.where(row < col, mixed, 0.0)
    lower = jnp.where(row > col, mixed, 0.0)
    first = jnp.concatenate([upper + upper.T, corner], axis=1)
    second = jnp.concatenate([corner.T, lower + lower.T], axis=1)
    return jnp.concatenate([first, second], axis=0)


def gram(left, right):
    return lax.dot_general(left, right, (((0,), (0,)), ((), ())), preferred_element_type=F32)


def kernel(
    tiles, var_size, samp_size, inv_total,
    geno_hbm, marg_hbm, start_hbm, limit_hbm, out,
    geno, halo, marg, start, limit_row, own, code, got, diag, diag_got,
    band_hi, band_lo, eff_hi, eff_lo, edge_code, edge_got, cross_code, cross_got,
    load_sem, geno_send, geno_recv, part_send, part_recv, cross_sem, edge_send, edge_recv,
):
    var = lax.axis_index("var")
    samp = lax.axis_index("samp")
    has_prev = var > 0
    has_next = var < var_size - 1
    prev, following = var - 1, var + 1
    peers = [lax.rem(samp + k, samp_size) for k in range(1, samp_size)]
    last = tiles - 1
    pieces, width = edge_code.shape[2], edge_code.shape[4]
    slices = [slice(c * width, (c + 1) * width) for c in range(pieces)]

    step = HALF + TILE
    cross_at = tiles * step - TILE
    total_rows = cross_at + TILE

    loads = []
    for t in range(tiles):
        cols = pl.ds(t * TILE, TILE)
        loads.append(pltpu.make_async_copy(geno_hbm.at[:, cols], geno.at[:, cols], load_sem.at[t]))
    loads.append(pltpu.make_async_copy(start_hbm, start, load_sem.at[tiles]))
    loads.append(pltpu.make_async_copy(marg_hbm, marg, load_sem.at[tiles + 1]))
    loads.append(pltpu.make_async_copy(limit_hbm, limit_row, load_sem.at[tiles + 2]))
    for copy in loads:
        copy.start()

    barrier = pltpu.get_barrier_semaphore()

    @pl.when(has_prev)
    def _():
        pl.semaphore_signal(barrier, inc=1, device_id={"var": prev}, device_id_type=MESH)

    @pl.when(has_next)
    def _():
        pl.semaphore_signal(barrier, inc=1, device_id={"var": following}, device_id_type=MESH)

    for peer in peers:
        pl.semaphore_signal(barrier, inc=1, device_id={"samp": peer}, device_id_type=MESH)
    pl.semaphore_wait(
        barrier, len(peers) + has_prev.astype(jnp.int32) + has_next.astype(jnp.int32)
    )

    depth = geno.shape[0] // CHUNKS

    def geno_copy(chunk):
        rows = pl.ds(chunk * depth, depth)
        return pltpu.make_async_remote_copy(
            src_ref=geno_hbm.at[rows, pl.ds(last * TILE, TILE)], dst_ref=halo.at[rows],
            send_sem=geno_send.at[chunk], recv_sem=geno_recv.at[chunk],
            device_id={"var": following}, device_id_type=MESH,
        )

    @pl.when(has_next)
    def _():
        for chunk in range(CHUNKS):
            geno_copy(chunk).start()

    def part_copy(k, message):
        if message == tiles + 1:
            src, dst = diag, diag_got.at[k]
        else:
            begin = message * step if message < tiles else cross_at
            rows = pl.ds(begin, TILE if message == tiles else HALF if message == last else step)
            src, dst = code.at[rows], got.at[k, rows]
        return pltpu.make_async_remote_copy(
            src_ref=src, dst_ref=dst,
            send_sem=part_send.at[k, message], recv_sem=part_recv.at[k, message],
            device_id={"samp": peers[k]}, device_id_type=MESH,
        )

    def send_part(message):
        for k in range(len(peers)):
            part_copy(k, message).start()

    diag[...] = jnp.zeros_like(diag)
    row, col = iota_pair(TILE)
    on_diagonal = row == col

    for t in range(tiles):
        if t == 0:
            loads[0].wait()
        if t + 1 < tiles:
            loads[t + 1].wait()
        reach = min(t + 2, tiles) * TILE
        product = gram(geno[:, t * TILE : (t + 1) * TILE], geno[:, t * TILE : reach])
        product = product * (inv_total * LD_SCALE)
        block = product[:, :TILE]
        diag[pl.ds(t, 1), :] = jnp.sum(jnp.where(on_diagonal, block, 0.0), axis=0, keepdims=True)
        begin = t * step
        packed = pack_symmetric(block)
        own[begin : begin + HALF] = packed
        code[begin : begin + HALF] = encode(packed)
        if t + 1 < tiles:
            beside = product[:, TILE:]
            own[begin + HALF : begin + step] = beside
            code[begin + HALF : begin + step] = encode(beside)
        if t == last:
            send_part(tiles + 1)
        send_part(t)

    for copy in loads[tiles:]:
        copy.wait()
    everything = slice(0, pieces * width)

    def place(sweep, slot, value, cols=everything):
        high, low = split(value)
        eff_hi[sweep, slot * TILE : (slot + 1) * TILE, cols] = high
        eff_lo[sweep, slot * TILE : (slot + 1) * TILE, cols] = low

    def edge_copy(sweep, side, piece):
        return pltpu.make_async_remote_copy(
            src_ref=edge_code.at[sweep, side, piece], dst_ref=edge_got.at[sweep, side, piece],
            send_sem=edge_send.at[sweep, side, piece], recv_sem=edge_recv.at[sweep, side, piece],
            device_id={"var": following if side else prev}, device_id_type=MESH,
        )

    def send_edge(sweep, side, piece):
        @pl.when(has_next if side else has_prev)
        def _():
            edge_copy(sweep, side, piece).start()

    def take_edge(sweep, side, piece):
        slot = 0 if side else tiles + 1
        exists = has_prev if side else has_next

        @pl.when(exists)
        def _():
            edge_copy(sweep, side, piece).wait_recv()
            place(sweep, slot, decode(edge_got[sweep, side, piece]), slices[piece])

        @pl.when(jnp.logical_not(exists))
        def _():
            place(sweep, slot, jnp.zeros((TILE, width), F32), slices[piece])

    for side, rows in ((1, slice(last * TILE, tiles * TILE)), (0, slice(0, TILE))):
        for piece in range(pieces):
            edge_code[0, side, piece] = encode(start[rows, slices[piece]])
            if side:
                send_edge(0, side, piece)
    for t in range(tiles):
        place(0, t + 1, start[t * TILE : (t + 1) * TILE])

    def summed(begin, size):
        value = own[begin : begin + size]
        for k in range(len(peers)):
            value = value + decode(got[k, begin : begin + size])
        return value

    def put(tile, slot, value):
        high, low = split(value)
        band_hi[tile, :, slot * TILE : (slot + 1) * TILE] = high
        band_lo[tile, :, slot * TILE : (slot + 1) * TILE] = low

    def applied(sweep, tile, first, count, cols=everything):
        across = slice(first * TILE, (first + count) * TILE)
        rows = slice((tile + first) * TILE, (tile + first + count) * TILE)
        high, low = band_hi[tile, :, across], band_lo[tile, :, across]
        near, rest = eff_hi[sweep, rows, cols], eff_lo[sweep, rows, cols]
        dot = functools.partial(jnp.dot, preferred_element_type=F32)
        return dot(high, near) + (dot(high, rest) + dot(low, near))

    def add_tile(t):
        for k in range(len(peers)):
            part_copy(k, t).wait_recv()
        begin = t * step
        put(t, 1, unpack_symmetric(summed(begin, HALF)) * (1.0 / LD_SCALE))
        if t + 1 < tiles:
            beside = summed(begin + HALF, TILE) * (1.0 / LD_SCALE)
            put(t, 2, beside)
            put(t + 1, 0, beside.T)

    def cross_step(now):
        @pl.when(jnp.logical_and(has_prev, now))
        def _():
            crossing = jnp.zeros((TILE, TILE), F32)
            for chunk in range(CHUNKS):
                rows = slice(chunk * depth, (chunk + 1) * depth)
                geno_copy(chunk).wait_recv()
                if chunk == CHUNKS - 1:
                    for piece in range(pieces):
                        edge_copy(0, 0, piece).start()
                crossing = crossing + gram(halo[rows], geno[rows, :TILE])
            crossing = crossing * (inv_total * LD_SCALE)
            own[cross_at:total_rows] = crossing
            code[cross_at:total_rows] = encode(crossing)
            send_part(tiles)

    nearby = lax.rem(var, 2) == 1
    cross_step(nearby)
    for t in range(last):
        add_tile(t)
    near_first = applied(0, 0, 1, 2)

    cross_step(jnp.logical_not(nearby))
    add_tile(last)
    for k in range(len(peers)):
        part_copy(k, tiles + 1).wait_recv()
    keep = []
    for t in range(tiles):
        whole = diag[pl.ds(t, 1), :]
        for k in range(len(peers)):
            whole = whole + diag_got[k, pl.ds(t, 1), :]
        column = jnp.sum(jnp.where(on_diagonal, whole, 0.0), axis=1, keepdims=True) * (1.0 / LD_SCALE)
        keep.append(1.0 / ((1.0 - shrinkage) * column + shrinkage))
    limit = limit_row[...]

    def finish(tile, combined, cols=everything):
        adjusted = marg[tile * TILE : (tile + 1) * TILE, cols] - (1.0 - shrinkage) * combined
        bound = limit[:, cols]
        return (adjusted - jnp.clip(adjusted, -bound, bound)) * keep[tile]

    for t in range(1, tiles - 1):
        place(1, t + 1, finish(t, applied(0, t, 0, 3)))
    near_last = applied(0, last, 0, 2)

    def back_copy():
        return pltpu.make_async_remote_copy(
            src_ref=cross_code, dst_ref=cross_got,
            send_sem=cross_sem.at[0], recv_sem=cross_sem.at[1],
            device_id={"var": prev}, device_id_type=MESH,
        )

    @pl.when(has_prev)
    def _():
        for k in range(len(peers)):
            part_copy(k, tiles).wait_recv()
        crossing = summed(cross_at, TILE)
        cross_code[...] = encode(crossing)
        back_copy().start()
        put(0, 0, crossing.T * (1.0 / LD_SCALE))

    @pl.when(jnp.logical_not(has_prev))
    def _():
        put(0, 0, jnp.zeros((TILE, TILE), F32))

    for piece, cols in enumerate(slices):
        take_edge(0, 1, piece)
        value = finish(0, near_first[:, cols] + applied(0, 0, 0, 1, cols), cols)
        edge_code[1, 0, piece] = encode(value)
        send_edge(1, 0, piece)
        place(1, 1, value, cols)

    for piece in range(pieces):
        take_edge(0, 0, piece)

    @pl.when(has_next)
    def _():
        back_copy().wait_recv()
        put(last, 2, decode(cross_got[...]) * (1.0 / LD_SCALE))

    @pl.when(jnp.logical_not(has_next))
    def _():
        put(last, 2, jnp.zeros((TILE, TILE), F32))

    for piece, cols in enumerate(slices):
        value = finish(last, near_last[:, cols] + applied(0, last, 2, 1, cols), cols)
        edge_code[1, 1, piece] = encode(value)
        send_edge(1, 1, piece)
        place(1, tiles, value, cols)

    for t in range(1, tiles - 1):
        out[t * TILE : (t + 1) * TILE] = finish(t, applied(1, t, 0, 3))
    near_last = applied(1, last, 0, 2)
    near_first = applied(1, 0, 1, 2)
    for piece, cols in enumerate(slices):
        take_edge(1, 0, piece)
        combined = near_last[:, cols] + applied(1, last, 2, 1, cols)
        out[last * TILE : tiles * TILE, cols] = finish(last, combined, cols)
    for piece, cols in enumerate(slices):
        take_edge(1, 1, piece)
        combined = near_first[:, cols] + applied(1, 0, 0, 1, cols)
        out[:TILE, cols] = finish(0, combined, cols)

    for k in range(len(peers)):
        for message in list(range(tiles)) + [tiles + 1]:
            part_copy(k, message).wait_send()

    @pl.when(has_prev)
    def _():
        for k in range(len(peers)):
            part_copy(k, tiles).wait_send()
        back_copy().wait_send()
        for sweep in range(SWEEPS):
            for piece in range(pieces):
                edge_copy(sweep, 0, piece).wait_send()

    @pl.when(has_next)
    def _():
        for chunk in range(CHUNKS):
            geno_copy(chunk).wait_send()
        for sweep in range(SWEEPS):
            for piece in range(pieces):
                edge_copy(sweep, 1, piece).wait_send()


def local(genotypes, marginal, start_effects, thresholds):
    samples, variants = genotypes.shape
    traits = marginal.shape[1]
    tiles = variants // TILE
    var_size, samp_size = lax.axis_size("var"), lax.axis_size("samp")
    others = samp_size - 1
    rows = tiles * (HALF + TILE)
    pieces = 1
    width = traits // pieces
    dma = pltpu.SemaphoreType.DMA
    body = functools.partial(
        kernel, tiles, var_size, samp_size, 1.0 / (samples * samp_size)
    )
    return pl.pallas_call(
        body,
        out_shape=jax.ShapeDtypeStruct((variants, traits), F32),
        in_specs=[pl.BlockSpec(memory_space=pltpu.HBM)] * 4,
        out_specs=pl.BlockSpec(memory_space=pltpu.VMEM),
        scratch_shapes=[
            pltpu.VMEM((samples, variants), BF16),
            pltpu.VMEM((samples, TILE), BF16),
            pltpu.VMEM((variants, traits), F32),
            pltpu.VMEM((variants, traits), F32),
            pltpu.VMEM((1, traits), F32),
            pltpu.VMEM((rows, TILE), F32),
            pltpu.VMEM((rows, TILE), BF16),
            pltpu.VMEM((others, rows, TILE), BF16),
            pltpu.VMEM((8, TILE), F32),
            pltpu.VMEM((others, 8, TILE), F32),
            pltpu.VMEM((tiles, TILE, 3 * TILE), BF16),
            pltpu.VMEM((tiles, TILE, 3 * TILE), BF16),
            pltpu.VMEM((SWEEPS, (tiles + 2) * TILE, traits), BF16),
            pltpu.VMEM((SWEEPS, (tiles + 2) * TILE, traits), BF16),
            pltpu.VMEM((SWEEPS, 2, pieces, TILE, width), BF16),
            pltpu.VMEM((SWEEPS, 2, pieces, TILE, width), BF16),
            pltpu.VMEM((TILE, TILE), BF16),
            pltpu.VMEM((TILE, TILE), BF16),
            dma((tiles + 3,)),
            dma((CHUNKS,)),
            dma((CHUNKS,)),
            dma((others, tiles + 2)),
            dma((others, tiles + 2)),
            dma((2,)),
            dma((SWEEPS, 2, pieces)),
            dma((SWEEPS, 2, pieces)),
        ],
        compiler_params=pltpu.CompilerParams(
            collective_id=0, has_side_effects=True, vmem_limit_bytes=VMEM_BYTES
        ),
    )(*(
        pltpu.with_memory_space_constraint(array, pltpu.HBM)
        for array in (genotypes, marginal, start_effects, thresholds[None, :])
    ))


def solution(mesh):
    in_specs = (P("samp", "var"), P("var", "samp"), P("var", "samp"), P("samp"))
    out_specs = P("var", "samp")
    return jax.shard_map(local, mesh=mesh, in_specs=in_specs, out_specs=out_specs, check_vma=False)
```
